128 devices in a mesh: tile: 16 (over z_hi, x, core), frame: 8 (over y, z_lo).
Axes of the slice: x: 4, y: 4, z: 4 (z_hi: 2, z_lo: 2; z = z_hi * 2 + z_lo), core: 2. Of those that a mesh axis runs over, the one named last changes fastest.
Arguments:
- frames: bfloat16 [8, 512, 512], P('frame', 'tile'), may hold values from -6 to 6
- row_shifts: int32 [512, 8], P('frame'), may hold values from -16 to 16, as said below
- column_shifts: int32 [512, 8], P('frame'), may hold values from -16 to 16, as said below
- frame_inverse_weight: float32 [8], replicated, may hold values from 0.05 to 0.5
- psf_rows: float32 [13], replicated, may hold values from 0.1 to 0.4
- psf_cols: float32 [13], replicated, may hold values from 0.1 to 0.4
Outputs:
- filtered: bfloat16 [512, 512, 512], P('frame', 'tile')
The draws below stay inside these ranges and needn't reach their ends.
Inputs may be any that keep to these rules, and one draw needn't show every extreme that they name: row_shifts[v, f] = floor(r_v * (2 f - 7) / 7) for an integer row rate r_v per velocity; both extremes are reached. column_shifts follows the same law with an integer column rate c_v per velocity; both extremes are reached; the rate pairs (r_v, c_v) are distinct across all 512 velocities.
All inputs are finite; a program needn't handle non-finite values.
Results may differ from the reference program's by a relative error of at most 0.005.
Values may be sent and summed in bfloat16 or wider, within the bound.
A program may use at most 64 MiB of HBM per device.

```python
import math
import jax
import jax.numpy as jnp
from jax import lax

COLS = 512
FRAMES = 8
VELOCITIES = 512
HALO = 16
RADIUS = 6
TAPS = 13
HEIGHT = 512


def pair_codes(key):
    key = jax.random.fold_in(key, 17)
    side = 2 * HALO + 1
    total = side * side
    others = jax.random.permutation(key, jnp.arange(1, total - 1, dtype=jnp.int32))
    planted = jnp.array([total - 1, 0], dtype=jnp.int32)
    return jnp.concatenate([planted, others[:VELOCITIES - 2]])


def motion_table(speed):
    moments = 2 * jnp.arange(FRAMES, dtype=jnp.int32) - (FRAMES - 1)
    return speed[:, None] * moments[None, :] // (FRAMES - 1)


def draw_row_shifts(key, part):
    codes = pair_codes(key)
    return motion_table(codes // (2 * HALO + 1) - HALO)


def draw_column_shifts(key, part):
    codes = pair_codes(key)
    return motion_table(codes % (2 * HALO + 1) - HALO)


def steps_of(stream_key, shape, cuts, smallest, high):
    level, own = 1.0, jax.random.fold_in(stream_key, 6)
    for position, shards_of in cuts:
        heights = jnp.exp(jax.random.uniform(jax.random.fold_in(own, position), (shards_of,), jnp.float32, smallest / len(cuts), high / len(cuts)))
        level = level * jnp.repeat(heights, shape[position] // shards_of).reshape([-1 if axis == position else 1 for axis in range(len(shape))])
    return level


def bell_draw(rng, shape, spread, most, shards=(), kind=jnp.bfloat16):
    gain = steps_of(rng, shape, shards, -0.22, 0.18) if shards else 1.0
    values = jax.random.normal(rng, shape, jnp.float32) * spread * gain
    return jnp.minimum(jnp.maximum(values, -most), most).astype(kind)


def setup_inputs(seed: int = 0) -> dict:
    key_of = jax.random.split(jax.random.key(seed), 7)
    return {
        "frames": bell_draw(key_of[0], (FRAMES, HEIGHT, COLS), 1.0, 6.0, ((0, 8), (1, 16))),
        "row_shifts": draw_row_shifts(jax.random.fold_in(key_of[6], 71), 0),
        "column_shifts": draw_column_shifts(jax.random.fold_in(key_of[6], 71), 0),
        "frame_inverse_weight": jnp.clip(jnp.exp(jax.random.uniform(key_of[3], (FRAMES,), jnp.float32, math.log(0.05), math.log(0.5))), 0.05, 0.5),
        "psf_rows": jnp.clip(jax.random.uniform(key_of[4], (TAPS,), jnp.float32, 0.1, 0.4), 0.1, 0.4),
        "psf_cols": jnp.clip(jax.random.uniform(key_of[5], (TAPS,), jnp.float32, 0.1, 0.4), 0.1, 0.4),
    }


def reference(frames, row_shifts, column_shifts, frame_inverse_weight, psf_rows, psf_cols):
    image_height = frames.shape[1]
    width = frames.shape[2]
    padded = jnp.pad(frames, ((0, 0), (HALO, HALO), (HALO, HALO)))

    def one_velocity(offsets):
        row_moves, col_moves = offsets

        def add_frame(index, total):
            frame_image = lax.dynamic_index_in_dim(padded, index, 0, keepdims=False)
            row_start = (HALO + row_moves[index]).astype(jnp.int32)
            col_start = (HALO + col_moves[index]).astype(jnp.int32)
            moved = lax.dynamic_slice(frame_image, (row_start, col_start), (image_height, width))
            return total + frame_inverse_weight[index] * moved.astype(jnp.float32)

        summed = lax.fori_loop(0, FRAMES, add_frame, jnp.zeros((image_height, width), jnp.float32))
        stack = summed.astype(jnp.bfloat16)
        extended = jnp.pad(stack, ((RADIUS, RADIUS), (0, 0)))
        rowpass = jnp.zeros((image_height, width), jnp.float32)
        for k in range(2 * RADIUS + 1):
            rowpass = rowpass + psf_rows[k] * extended[k:k + image_height].astype(jnp.float32)
        wide_rows = jnp.pad(rowpass, ((0, 0), (RADIUS, RADIUS)))
        result = jnp.zeros((image_height, width), jnp.float32)
        for k in range(2 * RADIUS + 1):
            result = result + psf_cols[k] * wide_rows[:, k:k + width]
        return result.astype(jnp.bfloat16)

    return lax.map(one_velocity, (row_shifts, column_shifts))
```

```python
import functools

import jax
import jax.numpy as jnp
from jax import lax
from jax.experimental import pallas as pl
from jax.experimental.pallas import tpu as pltpu
from jax.sharding import PartitionSpec as P

MESH = pl.DeviceIdType.MESH
HALO = 16
RADIUS = 6
TAPS = 2 * RADIUS + 1
FRAMES = 8
LANES = 128
STEP = 4
EDGE = 24
BAND = 32
TALL = BAND + 2 * EDGE
CUT = 40


def spans():
    out = []
    row = cut = 0
    for f in range(FRAMES):
        ends = [r * (2 * f - (FRAMES - 1)) // (FRAMES - 1) for r in (-HALO, HALO)]
        low, high = min(ends), max(ends)
        top = -(-(-low) // 8) * 8
        below = -(-high // 8) * 8
        count = high - low + STEP
        tall = top + BAND + below
        out.append((low, count, top, tall, row, cut))
        row += count * tall
        cut += count * CUT
    return out, row, cut


SPANS, TABLE_ROWS, CUT_ROWS = spans()


def gather_kernel(tiles, band_ref, all_ref, send, got, top_send, top_got, low_send, low_got):
    tile = lax.axis_index("tile")
    frame = lax.axis_index("frame")
    above, below = tile > 0, tile < tiles - 1
    peers = [lax.rem(frame + d, FRAMES) for d in range(1, FRAMES)]

    barrier = pltpu.get_barrier_semaphore()
    for peer in peers:
        pl.semaphore_signal(barrier, inc=1, device_id={"frame": peer}, device_id_type=MESH)

    @pl.when(above)
    def _():
        pl.semaphore_signal(barrier, inc=1, device_id={"tile": tile - 1}, device_id_type=MESH)

    @pl.when(below)
    def _():
        pl.semaphore_signal(barrier, inc=1, device_id={"tile": tile + 1}, device_id_type=MESH)

    pl.semaphore_wait(barrier, FRAMES - 1 + jnp.minimum(tile, 1) + jnp.minimum(tiles - 1 - tile, 1))

    def band_copy(peer, slot, source):
        return pltpu.make_async_remote_copy(
            src_ref=band_ref.at[0],
            dst_ref=all_ref.at[source, pl.ds(EDGE, BAND)],
            send_sem=send.at[slot],
            recv_sem=got.at[slot],
            device_id={"frame": peer},
            device_id_type=MESH,
        )

    def edge_copies(ref, slot, source):
        up = pltpu.make_async_remote_copy(
            src_ref=ref.at[pl.ds(0, EDGE)],
            dst_ref=all_ref.at[source, pl.ds(EDGE + BAND, EDGE)],
            send_sem=low_send.at[slot],
            recv_sem=low_got.at[slot],
            device_id={"tile": jnp.maximum(tile - 1, 0)},
            device_id_type=MESH,
        )
        down = pltpu.make_async_remote_copy(
            src_ref=ref.at[pl.ds(BAND - EDGE, EDGE)],
            dst_ref=all_ref.at[source, pl.ds(0, EDGE)],
            send_sem=top_send.at[slot],
            recv_sem=top_got.at[slot],
            device_id={"tile": jnp.minimum(tile + 1, tiles - 1)},
            device_id_type=MESH,
        )
        return up, down

    def forward(ref, slot, source):
        up, down = edge_copies(ref, slot, source)

        @pl.when(above)
        def _():
            up.start()

        @pl.when(below)
        def _():
            down.start()

    for d in range(1, FRAMES):
        band_copy(peers[d - 1], d, frame).start()
    forward(band_ref.at[0], 0, frame)
    all_ref[frame, pl.ds(EDGE, BAND)] = band_ref[0]

    @pl.when(jnp.logical_not(above))
    def _():
        all_ref[:, pl.ds(0, EDGE)] = jnp.zeros((FRAMES, EDGE, all_ref.shape[2]), all_ref.dtype)

    @pl.when(jnp.logical_not(below))
    def _():
        all_ref[:, pl.ds(EDGE + BAND, EDGE)] = jnp.zeros((FRAMES, EDGE, all_ref.shape[2]), all_ref.dtype)

    for d in range(1, FRAMES):
        source = lax.rem(frame + FRAMES - d, FRAMES)
        band_copy(peers[d - 1], d, source).wait_recv()
        forward(all_ref.at[source, pl.ds(EDGE, BAND)], d, source)
    for d in range(FRAMES):
        source = lax.rem(frame + FRAMES - d, FRAMES)
        up, down = edge_copies(all_ref.at[source, pl.ds(EDGE, BAND)], d, source)

        @pl.when(above)
        def _():
            up.wait_send()
            down.wait_recv()

        @pl.when(below)
        def _():
            down.wait_send()
            up.wait_recv()

    for d in range(1, FRAMES):
        band_copy(peers[d - 1], d, frame).wait_send()


def gather(tiles, frames):
    width = frames.shape[2]
    pair = pltpu.SemaphoreType.DMA((FRAMES,))
    return pl.pallas_call(
        functools.partial(gather_kernel, tiles),
        out_shape=jax.ShapeDtypeStruct((FRAMES, TALL, width), frames.dtype),
        in_specs=[pl.BlockSpec(memory_space=pltpu.VMEM)],
        out_specs=pl.BlockSpec(memory_space=pltpu.VMEM),
        scratch_shapes=[pair] * 6,
        compiler_params=pltpu.CompilerParams(collective_id=0, has_side_effects=True),
        name="gather",
    )(frames)


def stack_kernel(
    tile_of, tiles, group,
    row_ref, col_ref, weight_ref, psf_row_ref, psf_col_ref, all_ref, out_ref,
    table, cuts, order, banded, plain, coefs, sums,
):
    width = all_ref.shape[2]
    tile = tile_of()
    first, last = tile == 0, tile == tiles - 1
    edge = jnp.logical_or(first, last)

    @pl.when(pl.program_id(0) == 0)
    def _():
        x = lax.broadcasted_iota(jnp.int32, (width, LANES), 0)
        lane = lax.broadcasted_iota(jnp.int32, (width, LANES), 1)
        for j in range(STEP):
            order[:, j * LANES:(j + 1) * LANES] = jnp.where(x == STEP * lane + j, 1.0, 0.0).astype(jnp.bfloat16)

        banded[...] = jnp.zeros_like(banded)
        for j in range(STEP):
            for n in range(width // LANES):
                low = max(0, 32 * n - 16)
                high = min(LANES, 32 * n + 48)
                where = (
                    STEP * (lax.broadcasted_iota(jnp.int32, (high - low, LANES), 0) + low) + j
                    - lax.broadcasted_iota(jnp.int32, (high - low, LANES), 1) - n * LANES + RADIUS
                )
                block = jnp.zeros((high - low, LANES), jnp.float32)
                for k in range(TAPS):
                    block = jnp.where(where == k, psf_col_ref[k], block)
                banded[j * LANES + low:j * LANES + high, n * LANES:(n + 1) * LANES] = block.astype(jnp.bfloat16)

        s = lax.broadcasted_iota(jnp.int32, (8, LANES), 0)
        for u in range(RADIUS):
            top = jnp.zeros((8, LANES), jnp.float32)
            low = jnp.zeros((8, LANES), jnp.float32)
            for k in range(RADIUS):
                top = jnp.where(u - s == k, psf_row_ref[k], top)
                low = jnp.where(14 + u - s == k + RADIUS + 1, psf_row_ref[k + RADIUS + 1], low)
            coefs[u * 8:u * 8 + 8, :] = jnp.where(first, top, low)

        lanes = lax.broadcasted_iota(jnp.int32, (8, LANES), 1)

        def turned(value, q):
            if q == 0:
                return value
            moved = pltpu.roll(value, (-q) % LANES, 1)
            keep = lanes < LANES - q if q > 0 else lanes >= -q
            return jnp.where(jnp.broadcast_to(keep[:1], moved.shape), moved, 0.0)

        for f, (low, count, top, tall, row, cut) in enumerate(SPANS):
            picked = jnp.dot(all_ref[f], order[...], preferred_element_type=jnp.float32)
            for j in range(STEP):
                plain[j * TALL:(j + 1) * TALL, :] = picked[:, j * LANES:(j + 1) * LANES]
            taps = [psf_row_ref[k] * weight_ref[f] for k in range(TAPS)]
            for j in range(STEP):
                start = j * TALL + EDGE - top - RADIUS
                total = taps[0] * plain[start:start + tall, :]
                for k in range(1, TAPS):
                    total = total + taps[k] * plain[start + k:start + k + tall, :]
                for n in range(count):
                    if (low + n - j) % STEP == 0:
                        table[row + n * tall:row + (n + 1) * tall, :] = turned(total, (low + n - j) // STEP)

            @pl.when(edge)
            def _():
                for j in range(STEP):
                    start = j * TALL + jnp.where(first, EDGE - RADIUS - HALO, EDGE + BAND - HALO)
                    value = weight_ref[f] * plain[pl.ds(start, CUT), :]
                    for n in range(count):
                        if (low + n - j) % STEP == 0:
                            cuts[cut + n * CUT:cut + (n + 1) * CUT, :] = turned(value, (low + n - j) // STEP)

    def velocity(v, at_edge):
        vel = pl.program_id(0) * group + v
        rows, cut_rows = [], []
        for f, (low, count, top, tall, row, cut) in enumerate(SPANS):
            r = row_ref[f, vel]
            c = col_ref[f, vel] - low
            rows.append(c * tall + (r + (top + row)))
            cut_rows.append(c * CUT + (r + (HALO + cut)))
        for j in range(STEP):
            total = None
            for f, span in enumerate(SPANS):
                piece = table[pl.ds(rows[f] + j * span[3], BAND), :]
                total = piece if total is None else total + piece
            if at_edge:
                outside = None
                for f in range(FRAMES):
                    piece = cuts[pl.ds(cut_rows[f] + j * CUT, 8), :]
                    outside = piece if outside is None else outside + piece
                fix = None
                for u in range(RADIUS):
                    term = coefs[u * 8:u * 8 + 8, :] * jnp.broadcast_to(outside[u:u + 1], (8, LANES))
                    fix = term if fix is None else fix + term
                total = jnp.concatenate(
                    [
                        total[:8] - jnp.where(first, fix, 0.0),
                        total[8:24],
                        total[24:] - jnp.where(last, fix, 0.0),
                    ],
                    axis=0,
                )
            sums[pl.ds(pl.multiple_of(v * BAND, BAND), BAND), j * LANES:(j + 1) * LANES] = total.astype(jnp.bfloat16)

    @pl.when(edge)
    def _():
        @pl.loop(0, group)
        def _(v):
            velocity(v, True)

    @pl.when(jnp.logical_not(edge))
    def _():
        @pl.loop(0, group)
        def _(v):
            velocity(v, False)

    result = jnp.dot(sums[...], banded[...], preferred_element_type=jnp.float32)
    out_ref[...] = result.astype(out_ref.dtype).reshape(out_ref.shape)


def stacked(tile_of, tiles, everything, row_shifts, column_shifts, weights, psf_rows, psf_cols, group=16):
    vels = row_shifts.shape[0]
    width = everything.shape[2]
    smem = pl.BlockSpec(memory_space=pltpu.SMEM)
    return pl.pallas_call(
        functools.partial(stack_kernel, tile_of, tiles, group),
        out_shape=jax.ShapeDtypeStruct((vels, BAND, width), jnp.bfloat16),
        grid=(vels // group,),
        in_specs=[smem] * 5 + [pl.BlockSpec((FRAMES, TALL, width), lambda i: (0, 0, 0))],
        out_specs=pl.BlockSpec((group, BAND, width), lambda i: (i, 0, 0)),
        scratch_shapes=[
            pltpu.VMEM((TABLE_ROWS, LANES), jnp.float32),
            pltpu.VMEM((CUT_ROWS, LANES), jnp.float32),
            pltpu.VMEM((width, width), jnp.bfloat16),
            pltpu.VMEM((width, width), jnp.bfloat16),
            pltpu.VMEM((STEP * TALL, LANES), jnp.float32),
            pltpu.VMEM((RADIUS * 8, LANES), jnp.float32),
            pltpu.VMEM((group * BAND, width), jnp.bfloat16),
        ],
        compiler_params=pltpu.CompilerParams(vmem_limit_bytes=48 << 20),
        name="stack",
    )(row_shifts.T, column_shifts.T, weights, psf_rows, psf_cols, everything)


def shards(tiles, frames, row_shifts, column_shifts, frame_inverse_weight, psf_rows, psf_cols):
    everything = gather(tiles, frames)
    return stacked(
        lambda: lax.axis_index("tile"), tiles, everything,
        row_shifts, column_shifts, frame_inverse_weight, psf_rows, psf_cols,
    )


def solution(mesh):
    return jax.shard_map(
        functools.partial(shards, mesh.shape["tile"]),
        mesh=mesh,
        in_specs=(P("frame", "tile", None), P("frame", None), P("frame", None), P(), P(), P()),
        out_specs=P("frame", "tile", None),
        check_vma=False,
    )
```
